512 devices in a mesh: off: 16 (over z_lo, y), img: 32 (over x, z_hi, core).
Axes of the slice: x: 4, y: 4, z: 16 (z_hi: 4, z_lo: 4; z = z_hi * 4 + z_lo), core: 2. Of those that a mesh axis runs over, the one named last changes fastest.
Arguments:
- traces: bfloat16 [16384, 3072], P(('off', 'img')), may hold values from -6 to 6
- offset_bins: int32 [16384], P(('off', 'img')), may hold values from 0 to 15, as said below
- class_slots: int32 [16384], P(('off', 'img')), may hold values from 0 to 1, as said below
- weights: bfloat16 [16, 16384, 1024], P('off', 'img'), may hold values from -0.1875 to 0.1875
- band_start: int32 [16, 128], P('off', 'img'), may hold values from 0 to 1536
- smoothing: int32 [16, 128], P('off', 'img'), may hold values from 0 to 1
Outputs:
- migrated: bfloat16 [16, 16384, 1536], P('off', 'img')
The draws below stay inside these ranges and needn't reach their ends.
Inputs may be any that keep to these rules, and one draw needn't show every extreme that they name: `offset_bins`: in each aligned block of 32 traces every class is named by exactly 2 traces. Within each aligned block of 32 traces the pairs (offset_bins, class_slots) are all distinct.
All inputs are finite; a program needn't handle non-finite values.
Results may differ from the reference program's by a relative error of at most 0.005.
Values may be sent and summed in bfloat16 or wider, within the bound.
No kernel may reach another device: no remote copies, remote signals or barrier semaphores. Data moves between devices by JAX's collectives and lax.ppermute only.
A program may use at most 128 MiB of HBM per device.

```python
import jax
import jax.numpy as jnp
from jax import lax

NS = 3072
NT = 1536
NLEV = 2
CB = 128
TR_DEV = 32
CLASSES = 16
PER_CLASS = 2
NTR = 16384
CLASS_TR = 1024
NCOL = 16384
NBLK = 128
N_OFF = 16
N_IMG = 32


def trace_order(key):
    block_keys = jax.random.split(jax.random.fold_in(key, 11), NTR // TR_DEV)
    orders = jax.vmap(lambda one_key: jax.random.permutation(one_key, TR_DEV))(block_keys)
    return orders.reshape(NTR).astype(jnp.int32)


def draw_offset_bins(key, part):
    return trace_order(key) // PER_CLASS


def draw_class_slots(key, part):
    return trace_order(key) % PER_CLASS


def set_ends(array, stream_key, smallest, top_value):
    extent = array.shape
    index_at = [jax.random.randint(jax.random.fold_in(stream_key, axis), (), 0, extent[axis]) for axis in range(len(extent))]
    array = array.at[tuple(index_at)].set(smallest)
    longest = extent.index(max(extent))
    index_at[longest] = (index_at[longest] + 1) % extent[longest]
    return array.at[tuple(index_at)].set(top_value)


def block_scale(key, dims, cuts, least, high):
    factor_of = 1.0
    for axis_at, shards_of in cuts:
        steps = jax.random.uniform(jax.random.fold_in(jax.random.fold_in(key, 6), axis_at), (shards_of,), jnp.float32, least / len(cuts), high / len(cuts))
        factor_of = factor_of * jnp.repeat(jnp.exp(steps), dims[axis_at] // shards_of).reshape((-1,) + (1,) * (len(dims) - 1 - axis_at))
    return factor_of


def centred(rng, extent, scale, reach, cuts=(), kind=jnp.bfloat16):
    drawn = jax.random.normal(rng, extent, jnp.float32) * scale
    if len(cuts) > 0:
        drawn = block_scale(rng, extent, cuts, -0.22, 0.18) * drawn
    return jnp.clip(drawn, min=-reach, max=reach).astype(kind)


def setup_inputs(seed: int = 0) -> dict:
    keys = jax.random.split(jax.random.key(seed), 7)
    return {
        "traces": centred(keys[0], (NTR, NS), 1.0, 6.0, ((0, 512),)),
        "offset_bins": draw_offset_bins(jax.random.fold_in(keys[6], 71), 0),
        "class_slots": draw_class_slots(jax.random.fold_in(keys[6], 71), 0),
        "weights": centred(keys[3], (CLASSES, NCOL, CLASS_TR), CLASS_TR ** -0.5, 0.1875, ((0, 16), (1, 32))),
        "band_start": set_ends(jax.random.randint(keys[4], (CLASSES, NBLK), 0, NS - NT + 1), jax.random.fold_in(keys[4], 1), 0, NS - NT).astype(jnp.int32),
        "smoothing": set_ends(jax.random.randint(keys[5], (CLASSES, NBLK), 0, NLEV), jax.random.fold_in(keys[5], 1), 0, NLEV - 1).astype(jnp.int32),
    }


def filtered_levels(samples):
    values = samples.astype(jnp.float32)
    edges = [(0, 0)] * (values.ndim - 1)
    padded = jnp.pad(values, edges + [(1, 1)])
    boosted = values - 0.5 * (padded[..., :-2] + padded[..., 2:])
    widened = jnp.pad(boosted, edges + [(2, 2)])
    smoothed = (3.0 * boosted + 2.0 * (widened[..., 1:-3] + widened[..., 3:-1]) + widened[..., :-4] + widened[..., 4:]) / 9.0
    return jnp.stack([boosted, smoothed]).astype(jnp.bfloat16)


def reference(traces, offset_bins, class_slots, weights, band_start, smoothing):
    levels = filtered_levels(traces)
    rows_all = jnp.arange(NTR, dtype=jnp.int32)
    block_index = rows_all // TR_DEV
    source_off = block_index // N_IMG
    source_img = block_index % N_IMG
    position = (source_img * N_OFF + source_off) * PER_CLASS + class_slots
    targets = offset_bins * CLASS_TR + position
    ordered = jnp.zeros_like(levels).at[:, targets].set(levels)

    def one_block(flat_index):
        class_index = flat_index // NBLK
        block_number = flat_index % NBLK
        weight_block = lax.dynamic_slice(weights, (class_index, block_number * CB, jnp.int32(0)), (1, CB, CLASS_TR))[0]
        segment = lax.dynamic_slice(ordered, (smoothing[class_index, block_number], class_index * CLASS_TR, band_start[class_index, block_number]), (1, CLASS_TR, NT))[0]
        return jnp.dot(weight_block, segment, preferred_element_type=jnp.float32).astype(jnp.bfloat16)

    blocks = lax.map(one_block, jnp.arange(CLASSES * NBLK, dtype=jnp.int32))
    return blocks.reshape(CLASSES, NCOL, NT)
```

```python
import functools

import jax
import jax.numpy as jnp
from jax import lax
from jax.experimental import pallas as pl
from jax.experimental.pallas import tpu as pltpu
from jax.sharding import Mesh
from jax.sharding import PartitionSpec as P

NT = 1536
NS = 3072
CB = 128
LANES = 128
WINDOW = NT + 3 * LANES
PADDED = NS + 4 * LANES
STEP = 256
ROWS = 16


def ring(axis, count, hop):
    pairs = [(i, (i + hop) % count) for i in range(count)]
    return functools.partial(lax.ppermute, axis_name=axis, perm=pairs)


def lane_shift(values, left):
    width = values.shape[1]
    return pltpu.roll(values, left % width, 1)


def migrate_kernel(
    where_ref, band_ref, level_ref, weights_ref, *refs
):
    pieces, (out_ref, traces, product, sems) = refs[:10], refs[10:]
    me_x, me_c = where_ref[0], where_ref[1]

    copies = []
    for half in range(2):
        core = me_c if half == 0 else 1 - me_c
        own, below, above, far_low, far_high = pieces[5 * half : 5 * half + 5]
        across = lax.rem(me_x + 2, 4)
        places = [
            (own, traces.at[me_x, :, core]),
            (below, traces.at[lax.rem(me_x + 3, 4), :, core]),
            (above, traces.at[lax.rem(me_x + 1, 4), :, core]),
            (far_low, traces.at[across, 0:2, core]),
            (far_high, traces.at[across, 2:4, core]),
        ]
        for source, target in places:
            copy = pltpu.make_async_copy(source, target, sems.at[len(copies)])
            copy.start()
            copies.append(copy)

    rows = product.shape[0]
    product[:, :LANES] = jnp.zeros((rows, LANES), jnp.float32)
    product[:, LANES + NS :] = jnp.zeros((rows, PADDED - NS - LANES), jnp.float32)
    for copy in copies:
        copy.wait()

    def multiply(step, carry):
        at = pl.multiple_of(step * STEP, STEP)
        part = traces[:, :, :, :, pl.ds(at, STEP)].reshape(-1, STEP)
        to = pl.multiple_of(at + LANES, LANES)
        product[:, pl.ds(to, STEP)] = jnp.dot(
            weights_ref[...], part, preferred_element_type=jnp.float32
        )
        return carry

    lax.fori_loop(0, NS // STEP, multiply, 0)

    groups = CB // ROWS
    lane = lax.broadcasted_iota(jnp.int32, (ROWS, WINDOW), 1)
    narrow = lax.broadcasted_iota(jnp.int32, (ROWS, LANES), 1)

    def finish(step, carry):
        block = step // groups
        start = band_ref[block]
        level = level_ref[block]
        tile = start // LANES
        fine = start - tile * LANES
        first = pl.multiple_of(tile * LANES, LANES)
        row = pl.multiple_of(step * ROWS, ROWS)
        raw = product[pl.ds(row, ROWS), pl.ds(first, WINDOW)]
        boosted = raw - 0.5 * (lane_shift(raw, 1) + lane_shift(raw, -1))
        time = lane + (first - LANES)
        boosted = jnp.where((time >= 0) & (time < NS), boosted, 0.0)
        box = boosted + (lane_shift(boosted, 1) + lane_shift(boosted, -1))
        wide = box + (lane_shift(box, 1) + lane_shift(box, -1))
        picked = jnp.where(level > 0, wide * (1.0 / 9.0), boosted)
        back = lax.rem(LANES - fine, LANES)
        turned = [
            pltpu.roll(picked[:, k * LANES : (k + 1) * LANES], back, 1)
            for k in range(1, NT // LANES + 2)
        ]
        keep = narrow < LANES - fine
        for k in range(NT // LANES):
            out_ref[pl.ds(row, ROWS), k * LANES : (k + 1) * LANES] = jnp.where(
                keep, turned[k], turned[k + 1]
            ).astype(out_ref.dtype)
        return carry

    lax.fori_loop(0, rows // ROWS, finish, 0)


def migrate(where, band_start, smoothing, weights, pieces):
    rows = weights.shape[0]
    smem = pl.BlockSpec(memory_space=pltpu.SMEM)
    vmem = pl.BlockSpec(memory_space=pltpu.VMEM)
    anywhere = pl.BlockSpec(memory_space=pl.ANY)
    return pl.pallas_call(
        migrate_kernel,
        out_shape=jax.ShapeDtypeStruct((rows, NT), jnp.bfloat16),
        in_specs=[smem, smem, smem, vmem] + [anywhere] * len(pieces),
        out_specs=vmem,
        scratch_shapes=[
            pltpu.VMEM((4, 4, 2, 32, NS), jnp.bfloat16),
            pltpu.VMEM((rows, PADDED), jnp.float32),
            pltpu.SemaphoreType.DMA((len(pieces),)),
        ],
        compiler_params=pltpu.CompilerParams(vmem_limit_bytes=40 << 20),
        cost_estimate=pl.CostEstimate(
            flops=2 * rows * 1024 * NS, bytes_accessed=9 << 20, transcendentals=0
        ),
    )(where, band_start, smoothing, weights, *pieces)


def per_device(traces, offset_bins, class_slots, weights, band_start, smoothing):
    count = traces.shape[0]
    targets = offset_bins * 2 + class_slots
    chosen = targets[None, :] == jnp.arange(count, dtype=jnp.int32)[:, None]
    ordered = jnp.dot(
        chosen.astype(jnp.bfloat16), traces, preferred_element_type=jnp.float32
    ).astype(jnp.bfloat16)
    copies = jnp.broadcast_to(ordered, (4,) + ordered.shape).reshape(-1, NS)
    own = lax.all_to_all(
        copies, ("zh", "zl", "y"), split_axis=0, concat_axis=0, tiled=True
    ).reshape(4, 32, NS)
    up, down, swap = ring("x", 4, 1), ring("x", 4, 3), ring("c", 2, 1)
    below, above = up(own), down(own)
    far_low, far_high = up(below[:2]), down(above[2:])
    mine = [own, below, above, far_low, far_high]
    other = [swap(piece) for piece in mine]
    where = jnp.stack([lax.axis_index("x"), lax.axis_index("c")]).astype(jnp.int32)
    result = migrate(where, band_start[0], smoothing[0], weights[0], mine + other)
    return result[None]


def solution(mesh):
    fine = Mesh(mesh.devices.reshape(4, 4, 4, 4, 2), ("zl", "y", "x", "zh", "c"))
    off, img = ("zl", "y"), ("x", "zh", "c")
    in_specs = (
        P(off + img, None),
        P(off + img),
        P(off + img),
        P(off, img, None),
        P(off, img),
        P(off, img),
    )
    return jax.shard_map(
        per_device, mesh=fine, in_specs=in_specs, out_specs=P(off, img, None), check_vma=False
    )
```

```python
import functools

import jax
import jax.numpy as jnp
from jax import lax
from jax.experimental import pallas as pl
from jax.experimental.pallas import tpu as pltpu
from jax.sharding import Mesh
from jax.sharding import PartitionSpec as P

NT = 1536
NS = 3072
CB = 128
LANES = 128
PADDED = NS + 4 * LANES
UNIT = 32
HALF = 48


def ring(axis, count, hop):
    pairs = [(i, (i + hop) % count) for i in range(count)]
    return functools.partial(lax.ppermute, axis_name=axis, perm=pairs)


def gather(piece, axes):
    return lax.all_gather(piece, axes, axis=0, tiled=True)


def spread(piece, first, last, target):
    moves = []
    row = first
    while row < last:
        stop = min(last, (row // UNIT + 1) * UNIT)
        block, low = row // UNIT, row % UNIT
        moves.append((piece.at[row - first : stop - first], target(block).at[low : low + stop - row]))
        row = stop
    return moves


def migrate_kernel(where_ref, band_ref, level_ref, weights_ref, early, *refs):
    pieces, (out_ref, traces, *products, sems) = refs[:10], refs[10:]
    me_x, me_z, me_c = where_ref[0], where_ref[1], where_ref[2]

    moves = [(early, traces.at[:, me_z])]
    for half in range(2):
        core = me_c if half == 0 else 1 - me_c
        for slot, hop, first, last in (
            (0, 0, 0, 2 * HALF),
            (1, 3, 0, 2 * HALF),
            (2, 1, 0, 2 * HALF),
            (3, 2, 0, HALF),
            (4, 2, HALF, 2 * HALF),
        ):
            x = lax.rem(me_x + hop, 4)
            moves += spread(
                pieces[5 * half + slot],
                first,
                last,
                lambda block: traces.at[x, lax.rem(me_z + 1 + block, 4), core],
            )
    copies = []
    for at, (source, target) in enumerate(moves):
        copy = pltpu.make_async_copy(source, target, sems.at[at])
        copy.start()
        copies.append(copy)
    for copy in copies:
        copy.wait()

    lane = lax.broadcasted_iota(jnp.int32, (CB, LANES), 1)
    for block, product in enumerate(products):
        rows = slice(block * CB, (block + 1) * CB)
        product[:, LANES : LANES + NS] = jnp.dot(
            weights_ref[rows, :],
            traces[...].reshape(-1, NS),
            preferred_element_type=jnp.float32,
        )
        first = product[:, LANES : 2 * LANES][:, :1]
        last = product[:, NS : NS + LANES][:, LANES - 1 :]
        product[:, :LANES] = jnp.where(
            lane == LANES - 3, -2.0 * first, jnp.where(lane == LANES - 2, -first, 0.0)
        )
        product[:, LANES + NS : 2 * LANES + NS] = jnp.where(
            lane == 1, -last, jnp.where(lane == 2, -2.0 * last, 0.0)
        )
        product[:, 2 * LANES + NS :] = jnp.zeros((CB, 2 * LANES), jnp.float32)

        start = band_ref[block] + LANES
        smooth = level_ref[block] > 0
        reach = jnp.where(smooth, 3, 1)
        scale = jnp.where(smooth, 1.0 / 9.0, 1.0)
        turned, keeps = [], []
        for at in (start, start - reach, start + reach):
            tile = at // LANES
            fine = at - tile * LANES
            wide = product[:, pl.ds(pl.multiple_of(tile * LANES, LANES), NT + LANES)]
            back = lax.rem(LANES - fine, LANES)
            turned.append(
                [
                    pltpu.roll(wide[:, k * LANES : (k + 1) * LANES], back, 1)
                    for k in range(NT // LANES + 1)
                ]
            )
            keeps.append(lane < LANES - fine)
        for k in range(NT // LANES):
            middle, left, right = [
                jnp.where(keep, tiles[k], tiles[k + 1]) for keep, tiles in zip(keeps, turned)
            ]
            out_ref[rows, k * LANES : (k + 1) * LANES] = (
                (middle - 0.5 * (left + right)) * scale
            ).astype(out_ref.dtype)


def migrate(where, band_start, smoothing, weights, early, pieces):
    rows = weights.shape[0]
    smem = pl.BlockSpec(memory_space=pltpu.SMEM)
    vmem = pl.BlockSpec(memory_space=pltpu.VMEM)
    anywhere = pl.BlockSpec(memory_space=pl.ANY)
    return pl.pallas_call(
        migrate_kernel,
        out_shape=jax.ShapeDtypeStruct((rows, NT), jnp.bfloat16),
        in_specs=[smem, smem, smem, vmem, anywhere] + [anywhere] * len(pieces),
        out_specs=vmem,
        scratch_shapes=[pltpu.VMEM((4, 4, 2, UNIT, NS), jnp.bfloat16)]
        + [pltpu.VMEM((CB, PADDED), jnp.float32)] * (rows // CB)
        + [pltpu.SemaphoreType.DMA((32,))],
        compiler_params=pltpu.CompilerParams(vmem_limit_bytes=40 << 20),
        cost_estimate=pl.CostEstimate(
            flops=2 * rows * 1024 * NS, bytes_accessed=9 << 20, transcendentals=0
        ),
    )(where, band_start, smoothing, weights, early, *pieces)


def per_device(traces, offset_bins, class_slots, weights, band_start, smoothing):
    count = traces.shape[0]
    targets = offset_bins * 2 + class_slots
    chosen = targets[None, :] == jnp.arange(count, dtype=jnp.int32)[:, None]
    ordered = jnp.dot(
        chosen.astype(jnp.bfloat16), traces, preferred_element_type=jnp.float32
    ).astype(jnp.bfloat16)
    mine = lax.all_to_all(ordered, ("zl", "y"), split_axis=0, concat_axis=0, tiled=True)
    early = gather(mine, ("x", "c")).reshape(4, 2, UNIT, NS)
    planes = gather(mine, "zh")
    me_x, me_z, me_c = [lax.axis_index(axis) for axis in ("x", "zh", "c")]
    own = jnp.concatenate(
        [
            lax.dynamic_slice_in_dim(planes, lax.rem(me_z + hop, 4) * UNIT, UNIT)
            for hop in (1, 2, 3)
        ]
    )
    up, down, swap = ring("x", 4, 1), ring("x", 4, 3), ring("c", 2, 1)
    below, above = up(own), down(own)
    far_low, far_high = up(below[:HALF]), down(above[HALF:])
    pieces = [own, below, above, far_low, far_high]
    pieces += [swap(piece) for piece in pieces]
    where = jnp.stack([me_x, me_z, me_c]).astype(jnp.int32)
    return migrate(where, band_start[0], smoothing[0], weights[0], early, pieces)[None]


def solution(mesh):
    fine = Mesh(mesh.devices.reshape(4, 4, 4, 4, 2), ("zl", "y", "x", "zh", "c"))
    off, img = ("zl", "y"), ("x", "zh", "c")
    in_specs = (
        P(off + img, None),
        P(off + img),
        P(off + img),
        P(off, img, None),
        P(off, img),
        P(off, img),
    )
    return jax.shard_map(
        per_device, mesh=fine, in_specs=in_specs, out_specs=P(off, img, None), check_vma=False
    )
```

```python
import functools

import jax
import jax.numpy as jnp
from jax import lax
from jax.experimental import pallas as pl
from jax.experimental.pallas import tpu as pltpu
from jax.sharding import Mesh
from jax.sharding import PartitionSpec as P

NT = 1536
NS = 3072
CB = 128
LANES = 128
PADDED = NS + 4 * LANES
SPAN = NT + 2 * LANES


def x_ring(sign):
    pairs = []
    for x in range(4):
        for core in range(2):
            hop = sign if core == 0 else -sign
            pairs.append((2 * x + core, 2 * ((x + hop) % 4) + core))
    return functools.partial(lax.ppermute, axis_name=("x", "c"), perm=pairs)


def swap(piece):
    return lax.ppermute(piece, "c", [(0, 1), (1, 0)])


def arranged(weights_ref, x, me_c):
    old = lax.broadcasted_iota(jnp.int32, (2 * LANES, 2 * LANES), 0)
    new = lax.broadcasted_iota(jnp.int32, (2 * LANES, 2 * LANES), 1)
    core = jnp.where(new < LANES, me_c, 1 - me_c)
    source = (new % LANES) // 32 * 64 + core * 32 + new % 32
    chosen = jnp.where(old == source, 1.0, 0.0).astype(jnp.bfloat16)
    columns = pl.ds(pl.multiple_of(x * 2 * LANES, 2 * LANES), 2 * LANES)
    return jnp.dot(
        weights_ref[:, columns], chosen, preferred_element_type=jnp.float32
    ).astype(jnp.bfloat16)


def own_kernel(where_ref, weights_ref, *refs):
    pieces, (out_ref, sorted_ref) = refs[:-2], refs[-2:]
    me_x, me_c = where_ref[0], where_ref[1]
    nearest = me_x + 3 + 2 * me_c
    for slot, x in enumerate((me_x, nearest, nearest + 2, me_x + 2)):
        sorted_ref[:, slot * 2 * LANES : (slot + 1) * 2 * LANES] = arranged(
            weights_ref, lax.rem(x, 4), me_c
        )
    traces = jnp.concatenate([piece[...] for piece in pieces], axis=0)
    out_ref[...] = jnp.dot(
        sorted_ref[:, : 2 * LANES], traces, preferred_element_type=jnp.float32
    )


def near_kernel(weights_ref, product_ref, *refs):
    pieces, out_ref = refs[:-1], refs[-1]
    traces = jnp.concatenate([piece[...] for piece in pieces], axis=0)
    out_ref[...] = product_ref[...] + jnp.dot(
        weights_ref[:, 2 * LANES : 6 * LANES], traces, preferred_element_type=jnp.float32
    )


def far_kernel(band_ref, level_ref, weights_ref, near_ref, mine_ref, theirs_ref, out_ref, *products):
    lane = lax.broadcasted_iota(jnp.int32, (CB, LANES), 1)
    for block, product in enumerate(products):
        rows = slice(block * CB, (block + 1) * CB)
        at = jnp.clip((band_ref[block] - 3 + LANES) // LANES - 1, 0, (NS - SPAN) // LANES)
        span = pl.ds(pl.multiple_of(at * LANES, LANES), SPAN)
        traces = jnp.concatenate([mine_ref[:, span], theirs_ref[:, span]], axis=0)
        product[:, pl.ds(pl.multiple_of((at + 1) * LANES, LANES), SPAN)] = near_ref[
            rows, span
        ] + jnp.dot(
            weights_ref[rows, 6 * LANES :], traces, preferred_element_type=jnp.float32
        )
        first = product[:, LANES : 2 * LANES][:, :1]
        last = product[:, NS : NS + LANES][:, LANES - 1 :]
        product[:, :LANES] = jnp.where(
            lane == LANES - 3, -2.0 * first, jnp.where(lane == LANES - 2, -first, 0.0)
        )
        product[:, LANES + NS : 2 * LANES + NS] = jnp.where(
            lane == 1, -last, jnp.where(lane == 2, -2.0 * last, 0.0)
        )
        product[:, 2 * LANES + NS :] = jnp.zeros((CB, 2 * LANES), jnp.float32)

        start = band_ref[block] + LANES
        smooth = level_ref[block] > 0
        reach = jnp.where(smooth, 3, 1)
        scale = jnp.where(smooth, 1.0 / 9.0, 1.0)
        turned, keeps = [], []
        for at in (start, start - reach, start + reach):
            tile = at // LANES
            fine = at - tile * LANES
            wide = product[:, pl.ds(pl.multiple_of(tile * LANES, LANES), NT + LANES)]
            back = lax.rem(LANES - fine, LANES)
            turned.append(
                [
                    pltpu.roll(wide[:, k * LANES : (k + 1) * LANES], back, 1)
                    for k in range(NT // LANES + 1)
                ]
            )
            keeps.append(lane < LANES - fine)
        for k in range(NT // LANES):
            middle, left, right = [
                jnp.where(keep, tiles[k], tiles[k + 1]) for keep, tiles in zip(keeps, turned)
            ]
            out_ref[rows, k * LANES : (k + 1) * LANES] = (
                (middle - 0.5 * (left + right)) * scale
            ).astype(out_ref.dtype)


SMEM = pl.BlockSpec(memory_space=pltpu.SMEM)
VMEM = pl.BlockSpec(memory_space=pltpu.VMEM)


def kernel_call(body, outs, in_specs, depth, scratch=()):
    return pl.pallas_call(
        body,
        out_shape=outs,
        in_specs=in_specs,
        out_specs=jax.tree.map(lambda _: VMEM, outs),
        scratch_shapes=list(scratch),
        compiler_params=pltpu.CompilerParams(vmem_limit_bytes=16 << 20),
        cost_estimate=pl.CostEstimate(
            flops=4 * depth * NS, bytes_accessed=depth, transcendentals=0
        ),
    )


def per_device(traces, offset_bins, class_slots, weights, band_start, smoothing):
    count = traces.shape[0]
    targets = offset_bins * 2 + class_slots
    chosen = targets[None, :] == jnp.arange(count, dtype=jnp.int32)[:, None]
    ordered = jnp.dot(
        chosen.astype(jnp.bfloat16), traces, preferred_element_type=jnp.float32
    ).astype(jnp.bfloat16)
    mine = lax.all_to_all(ordered, ("zl", "y"), split_axis=0, concat_axis=0, tiled=True)
    own = lax.all_gather(mine, "zh", axis=0, tiled=True)
    forth, back = x_ring(1), x_ring(-1)
    first, second, own_other = forth(own), back(own), swap(own)
    weights = weights[0]
    rows = weights.shape[0]
    where = jnp.stack([lax.axis_index("x"), lax.axis_index("c")]).astype(jnp.int32)
    product = jax.ShapeDtypeStruct((rows, NS), jnp.float32)
    total, weights = kernel_call(
        own_kernel,
        (product, jax.ShapeDtypeStruct(weights.shape, weights.dtype)),
        [SMEM] + [VMEM] * 3,
        256,
    )(where, weights, own, own_other)
    first, total = lax.optimization_barrier((first, total))
    far = forth(first)
    pieces = [first, swap(second), second, swap(first)]
    far, total = lax.optimization_barrier((far, total))
    total = kernel_call(near_kernel, product, [VMEM] * 6, 512)(weights, total, *pieces)
    return kernel_call(
        far_kernel,
        jax.ShapeDtypeStruct((rows, NT), jnp.bfloat16),
        [SMEM] * 2 + [VMEM] * 4,
        256,
        [pltpu.VMEM((CB, PADDED), jnp.float32)] * (rows // CB),
    )(band_start[0], smoothing[0], weights, total, far, swap(far))[None]


def solution(mesh):
    fine = Mesh(mesh.devices.reshape(4, 4, 4, 4, 2), ("zl", "y", "x", "zh", "c"))
    off, img = ("zl", "y"), ("x", "zh", "c")
    in_specs = (
        P(off + img, None),
        P(off + img),
        P(off + img),
        P(off, img, None),
        P(off, img),
        P(off, img),
    )
    return jax.shard_map(
        per_device, mesh=fine, in_specs=in_specs, out_specs=P(off, img, None), check_vma=False
    )
```

```python
import functools

import jax
import jax.numpy as jnp
from jax import lax
from jax.experimental import pallas as pl
from jax.experimental.pallas import tpu as pltpu
from jax.sharding import Mesh
from jax.sharding import PartitionSpec as P

NT = 1536
NS = 3072
CB = 128
LANES = 128
PADDED = NS + 4 * LANES
SPAN = NT + 2 * LANES


def x_ring(sign):
    pairs = []
    for x in range(4):
        for core in range(2):
            hop = sign if core == 0 else -sign
            pairs.append((2 * x + core, 2 * ((x + hop) % 4) + core))
    return functools.partial(lax.ppermute, axis_name=("x", "c"), perm=pairs)


def swap(piece):
    return lax.ppermute(piece, "c", [(0, 1), (1, 0)])


def arranged(weights_ref, x, me_c):
    old = lax.broadcasted_iota(jnp.int32, (2 * LANES, 2 * LANES), 0)
    new = lax.broadcasted_iota(jnp.int32, (2 * LANES, 2 * LANES), 1)
    core = jnp.where(new < LANES, me_c, 1 - me_c)
    source = (new % LANES) // 32 * 64 + core * 32 + new % 32
    chosen = jnp.where(old == source, 1.0, 0.0).astype(jnp.bfloat16)
    columns = pl.ds(pl.multiple_of(x * 2 * LANES, 2 * LANES), 2 * LANES)
    return jnp.dot(
        weights_ref[:, columns], chosen, preferred_element_type=jnp.float32
    ).astype(jnp.bfloat16)


def own_kernel(where_ref, weights_ref, *refs):
    pieces, (out_ref, sorted_ref) = refs[:-2], refs[-2:]
    me_x, me_c = where_ref[0], where_ref[1]
    nearest = me_x + 3 + 2 * me_c
    for slot, x in enumerate((me_x, nearest, nearest + 2, me_x + 2)):
        sorted_ref[:, slot * 2 * LANES : (slot + 1) * 2 * LANES] = arranged(
            weights_ref, lax.rem(x, 4), me_c
        )
    traces = jnp.concatenate([piece[...] for piece in pieces], axis=0)
    out_ref[...] = jnp.dot(
        sorted_ref[:, : 2 * LANES], traces, preferred_element_type=jnp.float32
    )


def near_kernel(weights_ref, product_ref, *refs):
    pieces, out_ref = refs[:-1], refs[-1]
    traces = jnp.concatenate([piece[...] for piece in pieces], axis=0)
    out_ref[...] = product_ref[...] + jnp.dot(
        weights_ref[:, 2 * LANES : 6 * LANES], traces, preferred_element_type=jnp.float32
    )


def far_kernel(band_ref, level_ref, weights_ref, near_ref, mine_ref, theirs_ref, out_ref, *products):
    lane = lax.broadcasted_iota(jnp.int32, (CB, LANES), 1)
    for block, product in enumerate(products):
        rows = slice(block * CB, (block + 1) * CB)
        at = jnp.clip((band_ref[block] - 3 + LANES) // LANES - 1, 0, (NS - SPAN) // LANES)
        span = pl.ds(pl.multiple_of(at * LANES, LANES), SPAN)
        traces = jnp.concatenate([mine_ref[:, span], theirs_ref[:, span]], axis=0)
        product[:, pl.ds(pl.multiple_of((at + 1) * LANES, LANES), SPAN)] = near_ref[
            rows, span
        ] + jnp.dot(
            weights_ref[rows, 6 * LANES :], traces, preferred_element_type=jnp.float32
        )
        first = product[:, LANES : 2 * LANES][:, :1]
        last = product[:, NS : NS + LANES][:, LANES - 1 :]
        product[:, :LANES] = jnp.where(
            lane == LANES - 3, -2.0 * first, jnp.where(lane == LANES - 2, -first, 0.0)
        )
        product[:, LANES + NS : 2 * LANES + NS] = jnp.where(
            lane == 1, -last, jnp.where(lane == 2, -2.0 * last, 0.0)
        )
        product[:, 2 * LANES + NS :] = jnp.zeros((CB, 2 * LANES), jnp.float32)

        start = band_ref[block] + LANES
        smooth = level_ref[block] > 0
        reach = jnp.where(smooth, 3, 1)
        scale = jnp.where(smooth, 1.0 / 9.0, 1.0)
        turned, keeps = [], []
        for at in (start, start - reach, start + reach):
            tile = at // LANES
            fine = at - tile * LANES
            wide = product[:, pl.ds(pl.multiple_of(tile * LANES, LANES), NT + LANES)]
            back = lax.rem(LANES - fine, LANES)
            turned.append(
                [
                    pltpu.roll(wide[:, k * LANES : (k + 1) * LANES], back, 1)
                    for k in range(NT // LANES + 1)
                ]
            )
            keeps.append(lane < LANES - fine)
        for k in range(NT // LANES):
            middle, left, right = [
                jnp.where(keep, tiles[k], tiles[k + 1]) for keep, tiles in zip(keeps, turned)
            ]
            out_ref[rows, k * LANES : (k + 1) * LANES] = (
                (middle - 0.5 * (left + right)) * scale
            ).astype(out_ref.dtype)


SMEM = pl.BlockSpec(memory_space=pltpu.SMEM)
VMEM = pl.BlockSpec(memory_space=pltpu.VMEM)


def kernel_call(body, outs, in_specs, depth, scratch=()):
    return pl.pallas_call(
        body,
        out_shape=outs,
        in_specs=in_specs,
        out_specs=jax.tree.map(lambda _: VMEM, outs),
        scratch_shapes=list(scratch),
        compiler_params=pltpu.CompilerParams(vmem_limit_bytes=16 << 20),
        cost_estimate=pl.CostEstimate(
            flops=4 * depth * NS, bytes_accessed=depth, transcendentals=0
        ),
    )


def per_device(traces, offset_bins, class_slots, weights, band_start, smoothing):
    count = traces.shape[0]
    targets = offset_bins * 2 + class_slots
    chosen = targets[None, :] == jnp.arange(count, dtype=jnp.int32)[:, None]
    ordered = jnp.dot(
        chosen.astype(jnp.bfloat16), traces, preferred_element_type=jnp.float32
    ).astype(jnp.bfloat16)
    mine = lax.all_to_all(ordered, ("zl", "y"), split_axis=0, concat_axis=0, tiled=True)
    own = lax.all_gather(mine, "zh", axis=0, tiled=True)
    forth, back = x_ring(1), x_ring(-1)
    first, own_other = forth(own), swap(own)
    weights = weights[0]
    rows = weights.shape[0]
    where = jnp.stack([lax.axis_index("x"), lax.axis_index("c")]).astype(jnp.int32)
    product = jax.ShapeDtypeStruct((rows, NS), jnp.float32)
    total, weights = kernel_call(
        own_kernel,
        (product, jax.ShapeDtypeStruct(weights.shape, weights.dtype)),
        [SMEM] + [VMEM] * 3,
        256,
    )(where, weights, own, own_other)
    own, total = lax.optimization_barrier((own, total))
    second = back(own)
    first, total = lax.optimization_barrier((first, total))
    far = forth(first)
    pieces = [first, swap(second), second, swap(first)]
    far, total = lax.optimization_barrier((far, total))
    total = kernel_call(near_kernel, product, [VMEM] * 6, 512)(weights, total, *pieces)
    return kernel_call(
        far_kernel,
        jax.ShapeDtypeStruct((rows, NT), jnp.bfloat16),
        [SMEM] * 2 + [VMEM] * 4,
        256,
        [pltpu.VMEM((CB, PADDED), jnp.float32)] * (rows // CB),
    )(band_start[0], smoothing[0], weights, total, far, swap(far))[None]


def solution(mesh):
    fine = Mesh(mesh.devices.reshape(4, 4, 4, 4, 2), ("zl", "y", "x", "zh", "c"))
    off, img = ("zl", "y"), ("x", "zh", "c")
    in_specs = (
        P(off + img, None),
        P(off + img),
        P(off + img),
        P(off, img, None),
        P(off, img),
        P(off, img),
    )
    return jax.shard_map(
        per_device, mesh=fine, in_specs=in_specs, out_specs=P(off, img, None), check_vma=False
    )
```

```python
import functools

import jax
import jax.numpy as jnp
from jax import lax
from jax.experimental import pallas as pl
from jax.experimental.pallas import tpu as pltpu
from jax.sharding import Mesh
from jax.sharding import PartitionSpec as P

NT = 1536
NS = 3072
CB = 128
LANES = 128
PADDED = NS + 4 * LANES
SPAN = NT + 2 * LANES


def x_ring(sign):
    pairs = []
    for x in range(4):
        for core in range(2):
            hop = sign if core == 0 else -sign
            pairs.append((2 * x + core, 2 * ((x + hop) % 4) + core))
    return functools.partial(lax.ppermute, axis_name=("x", "c"), perm=pairs)


def swap(piece):
    return lax.ppermute(piece, "c", [(0, 1), (1, 0)])


def arranged(weights_ref, x, me_c):
    old = lax.broadcasted_iota(jnp.int32, (2 * LANES, 2 * LANES), 0)
    new = lax.broadcasted_iota(jnp.int32, (2 * LANES, 2 * LANES), 1)
    core = jnp.where(new < LANES, me_c, 1 - me_c)
    source = (new % LANES) // 32 * 64 + core * 32 + new % 32
    chosen = jnp.where(old == source, 1.0, 0.0).astype(jnp.bfloat16)
    columns = pl.ds(pl.multiple_of(x * 2 * LANES, 2 * LANES), 2 * LANES)
    return jnp.dot(
        weights_ref[:, columns], chosen, preferred_element_type=jnp.float32
    ).astype(jnp.bfloat16)


def own_kernel(where_ref, weights_ref, *refs):
    pieces, (out_ref, sorted_ref) = refs[:-2], refs[-2:]
    me_x, me_c = where_ref[0], where_ref[1]
    nearest = me_x + 3 + 2 * me_c
    for slot, x in enumerate((me_x, nearest, nearest + 2, me_x + 2)):
        sorted_ref[:, slot * 2 * LANES : (slot + 1) * 2 * LANES] = arranged(
            weights_ref, lax.rem(x, 4), me_c
        )
    traces = jnp.concatenate([piece[...] for piece in pieces], axis=0)
    out_ref[...] = jnp.dot(
        sorted_ref[:, : 2 * LANES], traces, preferred_element_type=jnp.float32
    )


def near_kernel(weights_ref, product_ref, *refs):
    pieces, out_ref = refs[:-1], refs[-1]
    traces = jnp.concatenate([piece[...] for piece in pieces], axis=0)
    out_ref[...] = product_ref[...] + jnp.dot(
        weights_ref[:, 2 * LANES : 6 * LANES], traces, preferred_element_type=jnp.float32
    )


def turned_taps(product, rows, start, reach, scale, out_ref):
    lane = lax.broadcasted_iota(jnp.int32, (CB, LANES), 1)
    turned, keeps = [], []
    for at in (start, start - reach, start + reach):
        tile = at // LANES
        fine = at - tile * LANES
        wide = product[:, pl.ds(pl.multiple_of(tile * LANES, LANES), NT + LANES)]
        back = lax.rem(LANES - fine, LANES)
        turned.append(
            [
                pltpu.roll(wide[:, k * LANES : (k + 1) * LANES], back, 1)
                for k in range(NT // LANES + 1)
            ]
        )
        keeps.append(lane < LANES - fine)
    for k in range(NT // LANES):
        middle, left, right = [
            jnp.where(keep, tiles[k], tiles[k + 1]) for keep, tiles in zip(keeps, turned)
        ]
        out_ref[rows, k * LANES : (k + 1) * LANES] = (
            (middle - 0.5 * (left + right)) * scale
        ).astype(out_ref.dtype)


def banded_taps(product, rows, start, reach, scale, out_ref):
    tile = (start - 3) // LANES
    fine = start - tile * LANES
    wide = product[:, pl.ds(pl.multiple_of(tile * LANES, LANES), SPAN)]
    high = wide.astype(jnp.bfloat16)
    low = (wide - high.astype(jnp.float32)).astype(jnp.bfloat16)
    offset = (
        lax.broadcasted_iota(jnp.int32, (4 * LANES, 2 * LANES), 0)
        - lax.broadcasted_iota(jnp.int32, (4 * LANES, 2 * LANES), 1)
        - fine
    )
    taps = jnp.where(
        offset == 0, 1.0, jnp.where((offset == reach) | (offset == -reach), -0.5, 0.0)
    ).astype(jnp.bfloat16)
    for at in range(0, NT, 2 * LANES):
        part = slice(at, at + 4 * LANES)
        result = jnp.dot(high[:, part], taps, preferred_element_type=jnp.float32) + jnp.dot(
            low[:, part], taps, preferred_element_type=jnp.float32
        )
        out_ref[rows, at : at + 2 * LANES] = (result * scale).astype(out_ref.dtype)


def far_kernel(band_ref, level_ref, weights_ref, near_ref, mine_ref, theirs_ref, out_hbm, *refs):
    *products, out_ref, sems = refs
    lane = lax.broadcasted_iota(jnp.int32, (CB, LANES), 1)
    copies = []
    for block, product in enumerate(products):
        rows = slice(block * CB, (block + 1) * CB)
        at = jnp.clip((band_ref[block] - 3 + LANES) // LANES - 1, 0, (NS - SPAN) // LANES)
        span = pl.ds(pl.multiple_of(at * LANES, LANES), SPAN)
        traces = jnp.concatenate([mine_ref[:, span], theirs_ref[:, span]], axis=0)
        product[:, pl.ds(pl.multiple_of((at + 1) * LANES, LANES), SPAN)] = near_ref[
            rows, span
        ] + jnp.dot(
            weights_ref[rows, 6 * LANES :], traces, preferred_element_type=jnp.float32
        )
        first = product[:, LANES : 2 * LANES][:, :1]
        last = product[:, NS : NS + LANES][:, LANES - 1 :]
        product[:, :LANES] = jnp.where(
            lane == LANES - 3, -2.0 * first, jnp.where(lane == LANES - 2, -first, 0.0)
        )
        product[:, LANES + NS : 2 * LANES + NS] = jnp.where(
            lane == 1, -last, jnp.where(lane == 2, -2.0 * last, 0.0)
        )
        product[:, 2 * LANES + NS :] = jnp.zeros((CB, 2 * LANES), jnp.float32)
        smooth = level_ref[block] > 0
        taps = turned_taps if block % 2 == 0 else banded_taps
        taps(
            product,
            rows,
            band_ref[block] + LANES,
            jnp.where(smooth, 3, 1),
            jnp.where(smooth, 1.0 / 9.0, 1.0),
            out_ref,
        )
        copy = pltpu.make_async_copy(out_ref.at[rows], out_hbm.at[rows], sems.at[block])
        copy.start()
        copies.append(copy)
    for copy in copies:
        copy.wait()


SMEM = pl.BlockSpec(memory_space=pltpu.SMEM)
VMEM = pl.BlockSpec(memory_space=pltpu.VMEM)


def kernel_call(body, outs, in_specs, depth, scratch=(), place=VMEM):
    return pl.pallas_call(
        body,
        out_shape=outs,
        in_specs=in_specs,
        out_specs=jax.tree.map(lambda _: place, outs),
        scratch_shapes=list(scratch),
        compiler_params=pltpu.CompilerParams(vmem_limit_bytes=16 << 20),
        cost_estimate=pl.CostEstimate(
            flops=4 * depth * NS, bytes_accessed=depth, transcendentals=0
        ),
    )


def per_device(traces, offset_bins, class_slots, weights, band_start, smoothing):
    count = traces.shape[0]
    targets = offset_bins * 2 + class_slots
    chosen = targets[None, :] == jnp.arange(count, dtype=jnp.int32)[:, None]
    ordered = jnp.dot(
        chosen.astype(jnp.bfloat16), traces, preferred_element_type=jnp.float32
    ).astype(jnp.bfloat16)
    mine = lax.all_to_all(ordered, ("zl", "y"), split_axis=0, concat_axis=0, tiled=True)
    own = lax.all_gather(mine, "zh", axis=0, tiled=True)
    forth, back = x_ring(1), x_ring(-1)
    first, own_other = forth(own), swap(own)
    weights = weights[0]
    rows = weights.shape[0]
    where = jnp.stack([lax.axis_index("x"), lax.axis_index("c")]).astype(jnp.int32)
    product = jax.ShapeDtypeStruct((rows, NS), jnp.float32)
    total, weights = kernel_call(
        own_kernel,
        (product, jax.ShapeDtypeStruct(weights.shape, weights.dtype)),
        [SMEM] + [VMEM] * 3,
        256,
    )(where, weights, own, own_other)
    own, total = lax.optimization_barrier((own, total))
    second = back(own)
    first, total = lax.optimization_barrier((first, total))
    far = forth(first)
    pieces = [first, swap(second), second, swap(first)]
    far, total = lax.optimization_barrier((far, total))
    total = kernel_call(near_kernel, product, [VMEM] * 6, 512)(weights, total, *pieces)
    return kernel_call(
        far_kernel,
        jax.ShapeDtypeStruct((rows, NT), jnp.bfloat16),
        [SMEM] * 2 + [VMEM] * 4,
        256,
        [pltpu.VMEM((CB, PADDED), jnp.float32)] * (rows // CB)
        + [pltpu.VMEM((rows, NT), jnp.bfloat16), pltpu.SemaphoreType.DMA((rows // CB,))],
        pl.BlockSpec(memory_space=pl.ANY),
    )(band_start[0], smoothing[0], weights, total, far, swap(far))[None]


def solution(mesh):
    fine = Mesh(mesh.devices.reshape(4, 4, 4, 4, 2), ("zl", "y", "x", "zh", "c"))
    off, img = ("zl", "y"), ("x", "zh", "c")
    in_specs = (
        P(off + img, None),
        P(off + img),
        P(off + img),
        P(off, img, None),
        P(off, img),
        P(off, img),
    )
    return jax.shard_map(
        per_device, mesh=fine, in_specs=in_specs, out_specs=P(off, img, None), check_vma=False
    )
```

```python
import functools

import jax
import jax.numpy as jnp
from jax import lax
from jax.experimental import pallas as pl
from jax.experimental.pallas import tpu as pltpu
from jax.sharding import Mesh
from jax.sharding import PartitionSpec as P

NT = 1536
NS = 3072
CB = 128
LANES = 128
PADDED = NS + 4 * LANES
SPAN = NT + 2 * LANES


def x_ring(sign):
    pairs = []
    for x in range(4):
        for core in range(2):
            hop = sign if core == 0 else -sign
            pairs.append((2 * x + core, 2 * ((x + hop) % 4) + core))
    return functools.partial(lax.ppermute, axis_name=("x", "c"), perm=pairs)


def swap(piece):
    return lax.ppermute(piece, "c", [(0, 1), (1, 0)])


def arranged(weights_ref, x, me_c):
    old = lax.broadcasted_iota(jnp.int32, (2 * LANES, 2 * LANES), 0)
    new = lax.broadcasted_iota(jnp.int32, (2 * LANES, 2 * LANES), 1)
    core = jnp.where(new < LANES, me_c, 1 - me_c)
    source = (new % LANES) // 32 * 64 + core * 32 + new % 32
    chosen = jnp.where(old == source, 1.0, 0.0).astype(jnp.bfloat16)
    columns = pl.ds(pl.multiple_of(x * 2 * LANES, 2 * LANES), 2 * LANES)
    return jnp.dot(
        weights_ref[:, columns], chosen, preferred_element_type=jnp.float32
    ).astype(jnp.bfloat16)


def own_kernel(where_ref, weights_ref, *refs):
    pieces, (out_ref, sorted_ref) = refs[:-2], refs[-2:]
    me_x, me_c = where_ref[0], where_ref[1]
    nearest = me_x + 3 + 2 * me_c
    for slot, x in enumerate((me_x, nearest, nearest + 2, me_x + 2)):
        sorted_ref[:, slot * 2 * LANES : (slot + 1) * 2 * LANES] = arranged(
            weights_ref, lax.rem(x, 4), me_c
        )
    traces = jnp.concatenate([piece[...] for piece in pieces], axis=0)
    out_ref[...] = jnp.dot(
        sorted_ref[:, : 2 * LANES], traces, preferred_element_type=jnp.float32
    )


def near_kernel(weights_ref, product_ref, *refs):
    pieces, out_ref = refs[:-1], refs[-1]
    traces = jnp.concatenate([piece[...] for piece in pieces], axis=0)
    out_ref[...] = product_ref[...] + jnp.dot(
        weights_ref[:, 2 * LANES : 6 * LANES], traces, preferred_element_type=jnp.float32
    )


def turned_taps(product, rows, start, reach, scale, out_ref):
    lane = lax.broadcasted_iota(jnp.int32, (CB, LANES), 1)
    turned, keeps = [], []
    for at in (start, start - reach, start + reach):
        tile = at // LANES
        fine = at - tile * LANES
        wide = product[:, pl.ds(pl.multiple_of(tile * LANES, LANES), NT + LANES)]
        back = lax.rem(LANES - fine, LANES)
        turned.append(
            [
                pltpu.roll(wide[:, k * LANES : (k + 1) * LANES], back, 1)
                for k in range(NT // LANES + 1)
            ]
        )
        keeps.append(lane < LANES - fine)
    for k in range(NT // LANES):
        middle, left, right = [
            jnp.where(keep, tiles[k], tiles[k + 1]) for keep, tiles in zip(keeps, turned)
        ]
        out_ref[rows, k * LANES : (k + 1) * LANES] = (
            (middle - 0.5 * (left + right)) * scale
        ).astype(out_ref.dtype)


def banded_taps(product, rows, start, reach, scale, out_ref):
    tile = (start - 3) // LANES
    fine = start - tile * LANES
    wide = product[:, pl.ds(pl.multiple_of(tile * LANES, LANES), SPAN)]
    high = wide.astype(jnp.bfloat16)
    low = (wide - high.astype(jnp.float32)).astype(jnp.bfloat16)
    offset = (
        lax.broadcasted_iota(jnp.int32, (4 * LANES, 2 * LANES), 0)
        - lax.broadcasted_iota(jnp.int32, (4 * LANES, 2 * LANES), 1)
        - fine
    )
    taps = jnp.where(
        offset == 0, 1.0, jnp.where((offset == reach) | (offset == -reach), -0.5, 0.0)
    ).astype(jnp.bfloat16)
    for at in range(0, NT, 2 * LANES):
        part = slice(at, at + 4 * LANES)
        result = jnp.dot(high[:, part], taps, preferred_element_type=jnp.float32) + jnp.dot(
            low[:, part], taps, preferred_element_type=jnp.float32
        )
        out_ref[rows, at : at + 2 * LANES] = (result * scale).astype(out_ref.dtype)


def far_kernel(band_ref, level_ref, weights_ref, near_ref, mine_ref, theirs_ref, out_hbm, *refs):
    *products, out_ref, sems = refs
    lane = lax.broadcasted_iota(jnp.int32, (CB, LANES), 1)
    copies = []
    for block, product in enumerate(products):
        rows = slice(block * CB, (block + 1) * CB)
        at = jnp.clip((band_ref[block] - 3 + LANES) // LANES - 1, 0, (NS - SPAN) // LANES)
        span = pl.ds(pl.multiple_of(at * LANES, LANES), SPAN)
        traces = jnp.concatenate([mine_ref[:, span], theirs_ref[:, span]], axis=0)
        product[:, pl.ds(pl.multiple_of((at + 1) * LANES, LANES), SPAN)] = near_ref[
            rows, span
        ] + jnp.dot(
            weights_ref[rows, 6 * LANES :], traces, preferred_element_type=jnp.float32
        )
        first = product[:, LANES : 2 * LANES][:, :1]
        last = product[:, NS : NS + LANES][:, LANES - 1 :]
        product[:, :LANES] = jnp.where(
            lane == LANES - 3, -2.0 * first, jnp.where(lane == LANES - 2, -first, 0.0)
        )
        product[:, LANES + NS : 2 * LANES + NS] = jnp.where(
            lane == 1, -last, jnp.where(lane == 2, -2.0 * last, 0.0)
        )
        product[:, 2 * LANES + NS :] = jnp.zeros((CB, 2 * LANES), jnp.float32)
        smooth = level_ref[block] > 0
        taps = turned_taps if block % 2 == 0 else banded_taps
        taps(
            product,
            rows,
            band_ref[block] + LANES,
            jnp.where(smooth, 3, 1),
            jnp.where(smooth, 1.0 / 9.0, 1.0),
            out_ref,
        )
        copy = pltpu.make_async_copy(out_ref.at[rows], out_hbm.at[rows], sems.at[block])
        copy.start()
        copies.append(copy)
    for copy in copies:
        copy.wait()


SMEM = pl.BlockSpec(memory_space=pltpu.SMEM)
VMEM = pl.BlockSpec(memory_space=pltpu.VMEM)


def kernel_call(body, outs, in_specs, depth, scratch=(), place=VMEM):
    return pl.pallas_call(
        body,
        out_shape=outs,
        in_specs=in_specs,
        out_specs=jax.tree.map(lambda _: place, outs),
        scratch_shapes=list(scratch),
        compiler_params=pltpu.CompilerParams(vmem_limit_bytes=16 << 20),
        cost_estimate=pl.CostEstimate(
            flops=4 * depth * NS, bytes_accessed=depth, transcendentals=0
        ),
    )


def per_device(traces, offset_bins, class_slots, weights, band_start, smoothing):
    count = traces.shape[0]
    rank = lax.broadcasted_iota(jnp.int32, (count, count), 0)
    chosen = (offset_bins[None, :] == rank >> 1) & (class_slots[None, :] == rank & 1)
    ordered = jnp.dot(
        chosen.astype(jnp.bfloat16), traces, preferred_element_type=jnp.float32
    ).astype(jnp.bfloat16)
    mine = lax.all_to_all(ordered, ("zl", "y"), split_axis=0, concat_axis=0, tiled=True)
    own = lax.all_gather(mine, "zh", axis=0, tiled=True)
    forth, back = x_ring(1), x_ring(-1)
    first, own_other = forth(own), swap(own)
    weights = weights[0]
    rows = weights.shape[0]
    where = jnp.stack([lax.axis_index("x"), lax.axis_index("c")]).astype(jnp.int32)
    product = jax.ShapeDtypeStruct((rows, NS), jnp.float32)
    total, weights = kernel_call(
        own_kernel,
        (product, jax.ShapeDtypeStruct(weights.shape, weights.dtype)),
        [SMEM] + [VMEM] * 3,
        256,
    )(where, weights, own, own_other)
    own, total = lax.optimization_barrier((own, total))
    second = back(own)
    first, total = lax.optimization_barrier((first, total))
    far = forth(first)
    pieces = [first, swap(second), second, swap(first)]
    far, total = lax.optimization_barrier((far, total))
    total = kernel_call(near_kernel, product, [VMEM] * 6, 512)(weights, total, *pieces)
    return kernel_call(
        far_kernel,
        jax.ShapeDtypeStruct((rows, NT), jnp.bfloat16),
        [SMEM] * 2 + [VMEM] * 4,
        256,
        [pltpu.VMEM((CB, PADDED), jnp.float32)] * (rows // CB)
        + [pltpu.VMEM((rows, NT), jnp.bfloat16), pltpu.SemaphoreType.DMA((rows // CB,))],
        pl.BlockSpec(memory_space=pl.ANY),
    )(band_start[0], smoothing[0], weights, total, far, swap(far))[None]


def solution(mesh):
    fine = Mesh(mesh.devices.reshape(4, 4, 4, 4, 2), ("zl", "y", "x", "zh", "c"))
    off, img = ("zl", "y"), ("x", "zh", "c")
    in_specs = (
        P(off + img, None),
        P(off + img),
        P(off + img),
        P(off, img, None),
        P(off, img),
        P(off, img),
    )
    return jax.shard_map(
        per_device, mesh=fine, in_specs=in_specs, out_specs=P(off, img, None), check_vma=False
    )
```
